32 devices in a mesh: dp: 4 (over y, core), cells: 8 (over z, x).
Axes of the slice: x: 2, y: 2, z: 4, core: 2. Of those that a mesh axis runs over, the one named last changes fastest.
Arguments:
- jac_blocks: bfloat16 [32, 128, 8192], P('dp', None, 'cells'), may hold values from -6 to 6
- slot_cell_blocks: int32 [32, 64], P('dp', 'cells'), may hold values from 0 to 15, as said below
- live_counts: int32 [32, 8], P('dp', 'cells'), may hold values from 1 to 8, as said below
- eigen_basis: bfloat16 [16384, 1536], P('cells', 'dp'), may hold values from -0.0625 to 0.0625
- weights: float32 [4096], P(('dp', 'cells')), may hold values from 0.25 to 4
- residual: float32 [4096], P(('dp', 'cells')), may hold values from -6 to 6
Outputs:
- jq: float32 [4096, 1536], P(('dp', 'cells'))
- system: float32 [1536, 1536], P('cells')
- rhs: float32 [1536], P('cells')
The draws below stay inside these ranges and needn't reach their ends.
Inputs may be any that keep to these rules, and one draw needn't show every extreme that they name: `slot_cell_blocks`: within one data block and one slab, the 8 entries name distinct cell blocks; only the first live_counts entries are used. `live_counts`: every data block has 8 live slots in some slab.
All inputs are finite; a program needn't handle non-finite values.
Results may differ from the reference program's by a relative error of at most 0.0003.
Values may be sent and summed in bfloat16 or wider, within the bound.
A program may use at most 128 MiB of HBM per device.

```python
import math
import jax
import jax.numpy as jnp
from jax import lax

K = 1536
BLOCK = 128
SLOTS = 8
CB_DEV = 16
SLABS = 8
CELLS = 16384
NDATA = 4096
DBLOCKS = 32


def draw_slot_cell_blocks(key, part):
    keys = jax.random.split(key, DBLOCKS * SLABS)
    picks = jax.vmap(lambda k: jax.random.permutation(k, CB_DEV)[:SLOTS])(keys)
    return picks.reshape(DBLOCKS, SLABS * SLOTS).astype(jnp.int32)


def draw_live_counts(key, part):
    key_start = jax.random.fold_in(key, 11)
    key_center = jax.random.fold_in(key, 12)
    key_jitter = jax.random.fold_in(key, 13)
    region = jax.random.randint(key_start, (), 0, SLABS)
    spread = max(SLABS // 4, 1)
    centers = (region + jax.random.randint(key_center, (DBLOCKS, 1), 0, spread)) % SLABS
    slab_ids = jnp.arange(SLABS, dtype=jnp.int32)[None, :]
    gap = jnp.abs(slab_ids - centers)
    dist = jnp.minimum(gap, SLABS - gap)
    jitter = jax.random.randint(key_jitter, (DBLOCKS, SLABS), -1, 2)
    counts = SLOTS - dist * SLOTS // (SLABS // 2 + 1) + jitter
    counts = jnp.clip(counts, 1, SLOTS)
    counts = jnp.where(dist == 0, SLOTS, counts)
    return counts.astype(jnp.int32)


def block_levels(own_key, extent, cuts, low, top_value):
    def one(dim, shards_of):
        steps = jax.random.uniform(jax.random.fold_in(jax.random.fold_in(own_key, 6), dim), (shards_of,), jnp.float32, low / len(cuts), top_value / len(cuts))
        return jnp.repeat(jnp.exp(steps), extent[dim] // shards_of).reshape((-1,) + (1,) * (len(extent) - dim - 1))

    gain = one(*cuts[0])
    for cut in cuts[1:]:
        gain = gain * one(*cut)
    return gain


def gaussian(key, extent, scale, limit, pieces=(), held_as=jnp.bfloat16):
    array = scale * jax.random.normal(key, extent, jnp.float32)
    if pieces:
        array = array * block_levels(key, extent, pieces, -0.22, 0.18)
    return jnp.clip(array, -limit, limit).astype(held_as)


def setup_inputs(seed: int = 0) -> dict:
    key_list = jax.random.split(jax.random.key(seed), 7)
    jac_blocks = gaussian(key_list[0], (DBLOCKS, BLOCK, SLABS * SLOTS * BLOCK), 1.0, 6.0, ((0, 4), (2, 8)))
    slot_cell_blocks = draw_slot_cell_blocks(jax.random.fold_in(key_list[6], 71), 0)
    live_counts = draw_live_counts(jax.random.fold_in(key_list[6], 71), 0)
    eigen_basis = gaussian(key_list[3], (CELLS, K), (BLOCK * SLOTS * SLABS) ** -0.5, 0.0625, ((0, 8), (1, 4)))
    weights = jnp.clip(jnp.exp(math.log(4.0) - 2.7725887 * jax.random.uniform(key_list[4], (NDATA,), jnp.float32) ** block_levels(key_list[4], (NDATA,), ((0, 32),), -0.2, 0.2)), 0.25, 4.0)
    residual = gaussian(key_list[5], (NDATA,), 1.0, 6.0, ((0, 32),), jnp.float32)
    return {"jac_blocks": jac_blocks, "slot_cell_blocks": slot_cell_blocks, "live_counts": live_counts, "eigen_basis": eigen_basis, "weights": weights, "residual": residual}


def reference(jac_blocks, slot_cell_blocks, live_counts, eigen_basis, weights, residual):
    block_width = eigen_basis.shape[1]
    stacked_blocks = eigen_basis.reshape(CELLS // BLOCK, BLOCK, block_width)
    slot_ids = jnp.arange(SLABS * SLOTS, dtype=jnp.int32)
    slab_base = slot_ids // SLOTS * CB_DEV
    slot_pos = slot_ids % SLOTS

    def one_block(items):
        jacobian_row, column_range, active_slot = items
        retain_flag = (slot_pos < jnp.repeat(active_slot, SLOTS)).astype(jnp.bfloat16)
        masked_entries = (jacobian_row.reshape(BLOCK, SLABS * SLOTS, BLOCK) * retain_flag[None, :, None]).reshape(BLOCK, SLABS * SLOTS * BLOCK)
        selected_rows = stacked_blocks[(column_range + slab_base).astype(jnp.int32)].reshape(SLABS * SLOTS * BLOCK, block_width)
        return jnp.dot(masked_entries, selected_rows, preferred_element_type=jnp.float32)
    jq = lax.map(one_block, (jac_blocks, slot_cell_blocks, live_counts)).reshape(NDATA, block_width)
    weighted = jq * weights[:, None]
    gram = lax.dot_general(jq, weighted, (((0,), (0,)), ((), ())), precision=lax.Precision.HIGHEST) / NDATA
    system = gram + jnp.eye(block_width, dtype=jnp.float32)
    rhs = lax.dot_general(jq, weights * residual, (((0,), (0,)), ((), ())), precision=lax.Precision.HIGHEST) / math.sqrt(NDATA)
    return (jq, system, rhs)
```

```python
import functools
import math

import jax
import jax.numpy as jnp
from jax import lax
from jax.experimental import pallas as pl
from jax.experimental.pallas import tpu as pltpu
from jax.sharding import PartitionSpec as P

PIECES = 4


def fused(
    n_cells, ndata,
    slots, live, jac, basis, wcol, rcol,
    jq, system, rhs,
    g1, g2, g3, sel, xsend, xrecv, zrecv, u, v, gram, gxr, gzr, vx, vxr, vzr, sysb,
    b_s, b_r, x_s, x_r, z_s, z_r, u_s, u_r, v_s, v_r,
    gx_s, gx_r, gz_s, gz_r, vx_s, vx_r, vz_s, vz_r, s_s, s_r,
):
    f32 = jnp.float32
    half = n_cells // 2
    tile = jac.shape[1]
    slot_count = jac.shape[2] // tile
    width = basis.shape[2]
    depth = basis.shape[0]
    own_rows = gxr.shape[1]
    me, cell = lax.axis_index("dp"), lax.axis_index("cells")
    core, y = me % 2, me // 2
    core_peer = y * 2 + 1 - core
    y_peer = (1 - y) * 2 + core
    far_peer = (1 - y) * 2 + 1 - core
    sources = (me, core_peer, y_peer, far_peer)
    x, line = cell % 2, cell // 2
    x_cell = line * 2 + 1 - x

    def remote(src, dst, send, recv, dp, to_cell):
        return pltpu.make_async_remote_copy(
            src_ref=src, dst_ref=dst, send_sem=send, recv_sem=recv,
            device_id=(dp, to_cell), device_id_type=pl.DeviceIdType.MESH,
        )

    def lanes(source):
        return pl.ds(pl.multiple_of(source * width, 128), width)

    barrier = pltpu.get_barrier_semaphore()
    for dp, to_cell in ((core_peer, cell), (y_peer, cell), (me, x_cell)):
        pl.semaphore_signal(
            barrier, inc=1, device_id=(dp, to_cell), device_id_type=pl.DeviceIdType.MESH
        )

    @pl.loop(1, half)
    def _(k):
        pl.semaphore_signal(
            barrier, inc=1, device_id=(me, (line + k) % half * 2 + x),
            device_id_type=pl.DeviceIdType.MESH,
        )

    pl.semaphore_wait(barrier, 3 + half - 1)

    step = depth // PIECES

    def y_piece(p):
        rows = pl.ds(p * step, step)
        return remote(basis.at[rows], g2.at[rows], b_s.at[1 + p], b_r.at[1 + p], y_peer, cell)

    def on_piece(p):
        rows = pl.ds(p * step, step)
        return remote(
            g2.at[rows], g3.at[rows], b_s.at[1 + PIECES + p], b_r.at[1 + PIECES + p],
            core_peer, cell,
        )

    to_core = remote(basis, g1, b_s.at[0], b_r.at[0], core_peer, cell)
    for p in range(PIECES):
        y_piece(p).start()
    to_core.start()

    chunks = (basis, g1, g2, g3)

    def block_dot(r, b):
        for t in range(slot_count):
            rows = chunks[r][slots[b, t]]
            sel[t * tile:(t + 1) * tile, :] = rows * live[b, t].astype(rows.dtype)
        return jnp.dot(jac[b], sel[...], preferred_element_type=f32)

    def x_copy(r, j):
        return remote(
            xsend.at[r % 2, j], xrecv.at[r, j], x_s.at[r, j], x_r.at[r, j], me, x_cell
        )

    def z_copy(r, j):
        return remote(
            xrecv.at[r, j], zrecv.at[r, line], z_s.at[r, j], z_r.at[r, line], me, 2 * j + x
        )

    def send_x(r):
        @pl.loop(0, half)
        def _(j):
            value = block_dot(r, 2 * j + 1 - x)
            if r >= 2:
                x_copy(r - 2, j).wait_send()
            xsend[r % 2, j] = value
            x_copy(r, j).start()

    def send_z(r):
        @pl.loop(1, half + 1)
        def _(k):
            j = (line + k) % half
            value = block_dot(r, 2 * j + x)
            x_copy(r, j).wait_recv()
            xrecv[r, j] = xrecv[r, j] + value

            @pl.when(k < half)
            def _():
                z_copy(r, j).start()

    def pass_on(p):
        y_piece(p).wait_recv()
        on_piece(p).start()

    send_x(0)
    to_core.wait_recv()
    send_x(1)
    pass_on(0)
    pass_on(1)
    send_z(0)
    pass_on(2)
    pass_on(3)
    send_x(2)
    send_z(1)
    for p in range(PIECES):
        on_piece(p).wait_recv()
    send_x(3)
    send_z(2)
    send_z(3)

    def u_copy(r, to):
        at = u.at[:, 0:tile, lanes(sources[r])]
        dst = u.at[:, (1 + to) * tile:(2 + to) * tile, lanes(sources[r])]
        return remote(at, dst, u_s.at[to, r], u_r.at[to, r], (core_peer, y_peer)[to], cell)

    def u_on(r):
        source = (y_peer, far_peer, me, core_peer)[r]
        return remote(
            u.at[:, 2 * tile:3 * tile, lanes(source)], u.at[:, 3 * tile:4 * tile, lanes(source)],
            u_s.at[2, r], u_r.at[2, r], core_peer, cell,
        )

    for r in range(4):
        @pl.loop(1, half)
        def _(k):
            j = (line + k) % half
            remote(
                xrecv.at[r, j], zrecv.at[r, j], z_s.at[r, j], z_r.at[r, j], me, 2 * j + x
            ).wait_recv()
            xrecv[r, line] = xrecv[r, line] + zrecv[r, j]

        total = xrecv[r, line]
        jq[:, lanes(sources[r])] = total
        scaled = total * wcol[...]
        high = scaled.astype(jnp.bfloat16)
        u[0, 0:tile, lanes(sources[r])] = high
        u[1, 0:tile, lanes(sources[r])] = (scaled - high.astype(f32)).astype(jnp.bfloat16)
        v[0, :, lanes(sources[r])] = jnp.sum(
            (total * rcol[...]).reshape(tile // 8, 8, width), axis=0
        )
        u_copy(r, 1).start()
        u_copy(r, 0).start()

    v_core = remote(v.at[0], v.at[1], v_s.at[0], v_r.at[0], core_peer, cell)
    v_y = remote(v.at[0], v.at[2], v_s.at[1], v_r.at[1], y_peer, cell)
    v_on = remote(v.at[2], v.at[3], v_s.at[2], v_r.at[2], core_peer, cell)
    v_y.start()
    v_core.start()
    for r in range(4):
        u_copy(r, 1).wait_recv()
        u_on(r).start()
    v_y.wait_recv()
    v_on.start()
    for r in range(4):
        u_copy(r, 0).wait_recv()
        u_on(r).wait_recv()
    v_core.wait_recv()
    v_on.wait_recv()

    vx_copy = remote(vx.at[0], vxr, vx_s, vx_r, me, x_cell)
    vx[0] = v[0] + v[1] + v[2] + v[3]
    vx_copy.start()

    m_tile = 256

    @pl.loop(0, gram.shape[0] // m_tile)
    def _(m):
        at = pl.ds(pl.multiple_of(m * m_tile, m_tile), m_tile)

        def product(a, b):
            return lax.dot_general(
                u[a, :, at], u[b, :, lanes(me)], (((0,), (0,)), ((), ())),
                preferred_element_type=f32,
            )

        gram[at, :] = (product(0, 0) + (product(0, 1) + product(1, 0))) / ndata

    def rows_of(c):
        return pl.ds(pl.multiple_of(c * own_rows, 8), own_rows)

    def gx_copy(j):
        return remote(
            gram.at[rows_of(2 * j + 1 - x)], gxr.at[j], gx_s.at[j], gx_r.at[j], me, x_cell
        )

    def gz_copy(j):
        return remote(gxr.at[j], gzr.at[line], gz_s.at[j], gz_r.at[line], me, 2 * j + x)

    def vz_copy(j):
        return remote(vx.at[1], vzr.at[line], vz_s.at[j], vz_r.at[line], me, 2 * j + x)

    @pl.loop(1, half + 1)
    def _(k):
        gx_copy((line + k) % half).start()

    vx_copy.wait_recv()
    vx[1] = vx[0] + vxr[...]

    @pl.loop(1, half)
    def _(k):
        vz_copy((line + k) % half).start()

    @pl.loop(1, half + 1)
    def _(k):
        j = (line + k) % half
        gx_copy(j).wait_recv()
        gxr[j] = gxr[j] + gram[rows_of(2 * j + x), :]

        @pl.when(k < half)
        def _():
            gz_copy(j).start()

    vx[2] = vx[1]
    sysb[0] = gxr[line]

    @pl.loop(1, half)
    def _(k):
        j = (line + k) % half
        remote(
            vx.at[1], vzr.at[j], vz_s.at[j], vz_r.at[j], me, 2 * j + x
        ).wait_recv()
        vx[2] = vx[2] + vzr[j]
        remote(
            gxr.at[j], gzr.at[j], gz_s.at[j], gz_r.at[j], me, 2 * j + x
        ).wait_recv()
        sysb[0] = sysb[0] + gzr[j]

    s_y = remote(sysb.at[0], sysb.at[2], s_s.at[1], s_r.at[1], y_peer, cell)
    s_core = remote(sysb.at[0], sysb.at[1], s_s.at[0], s_r.at[0], core_peer, cell)
    s_on = remote(sysb.at[2], sysb.at[3], s_s.at[2], s_r.at[2], core_peer, cell)
    s_y.start()
    s_core.start()
    rhs[...] = jnp.sum(vx[2], axis=0, keepdims=True) / math.sqrt(ndata)

    def finish(r):
        shape = (own_rows, width)
        row = lax.broadcasted_iota(jnp.int32, shape, 0) + cell * own_rows
        column = lax.broadcasted_iota(jnp.int32, shape, 1) + sources[r] * width
        system[:, lanes(sources[r])] = sysb[r] + (row == column).astype(f32)

    finish(0)
    s_core.wait_recv()
    finish(1)
    s_y.wait_recv()
    s_on.start()
    finish(2)
    s_on.wait_recv()
    finish(3)

    to_core.wait_send()
    for p in range(PIECES):
        y_piece(p).wait_send()
        on_piece(p).wait_send()
    for r in range(4):
        u_copy(r, 0).wait_send()
        u_copy(r, 1).wait_send()
        u_on(r).wait_send()
    for copy in (v_core, v_y, v_on, vx_copy, s_y, s_core, s_on):
        copy.wait_send()

    @pl.loop(1, half + 1)
    def _(k):
        j = (line + k) % half
        x_copy(2, j).wait_send()
        x_copy(3, j).wait_send()
        gx_copy(j).wait_send()

        @pl.when(k < half)
        def _():
            for r in range(4):
                z_copy(r, j).wait_send()
            gz_copy(j).wait_send()
            vz_copy(j).wait_send()


def on_device(jac_blocks, slot_cell_blocks, live_counts, eigen_basis, weights, residual):
    n_cells = lax.axis_size("cells")
    n_groups = lax.axis_size("dp")
    half = n_cells // 2
    tile = jac_blocks.shape[1]
    depth, width = eigen_basis.shape
    full = width * n_groups
    rows_here = full // n_cells
    ndata = weights.shape[0] * n_cells * n_groups
    assert n_groups == 4 and n_cells % 2 == 0
    assert jac_blocks.shape[0] == n_cells and weights.shape[0] == tile
    is_live = (lax.iota(jnp.int32, slot_cell_blocks.shape[1]) < live_counts).astype(jnp.float32)
    wcol = jnp.sqrt(weights)[:, None]
    rcol = (weights * residual)[:, None]
    f32, bf16 = jnp.float32, jnp.bfloat16
    vmem, smem = (pl.BlockSpec(memory_space=s) for s in (pltpu.VMEM, pltpu.SMEM))

    def sems(*shape):
        return [pltpu.SemaphoreType.DMA(shape)] * 2

    jq, system, rhs = pl.pallas_call(
        functools.partial(fused, n_cells, ndata),
        out_shape=(
            jax.ShapeDtypeStruct((tile, full), f32),
            jax.ShapeDtypeStruct((rows_here, full), f32),
            jax.ShapeDtypeStruct((1, full), f32),
        ),
        in_specs=[smem, smem, vmem, vmem, vmem, vmem],
        out_specs=(vmem, vmem, vmem),
        scratch_shapes=[
            pltpu.VMEM((depth // tile, tile, width), bf16),
            pltpu.VMEM((depth // tile, tile, width), bf16),
            pltpu.VMEM((depth // tile, tile, width), bf16),
            pltpu.VMEM((jac_blocks.shape[2], width), bf16),
            pltpu.VMEM((2, half, tile, width), f32),
            pltpu.VMEM((4, half, tile, width), f32),
            pltpu.VMEM((4, half, tile, width), f32),
            pltpu.VMEM((2, 4 * tile, full), bf16),
            pltpu.VMEM((4, 8, full), f32),
            pltpu.VMEM((full, width), f32),
            pltpu.VMEM((half, rows_here, width), f32),
            pltpu.VMEM((half, rows_here, width), f32),
            pltpu.VMEM((3, 8, full), f32),
            pltpu.VMEM((8, full), f32),
            pltpu.VMEM((half, 8, full), f32),
            pltpu.VMEM((4, rows_here, width), f32),
            *sems(1 + 2 * PIECES), *sems(4, half), *sems(4, half), *sems(3, 4), *sems(3),
            *sems(half), *sems(half), *sems(), *sems(half), *sems(3),
        ],
        compiler_params=pltpu.CompilerParams(
            collective_id=0, has_side_effects=True, vmem_limit_bytes=60 * 1024 * 1024
        ),
    )(
        slot_cell_blocks, is_live, jac_blocks,
        eigen_basis.reshape(depth // tile, tile, width), wcol, rcol,
    )
    start = lax.axis_index("cells") * rows_here
    return jq, system, lax.dynamic_slice(rhs[0], (start,), (rows_here,))


def solution(mesh):
    placed = (
        P("dp", None, "cells"),
        P("dp", "cells"),
        P("dp", "cells"),
        P("cells", "dp"),
        P(("dp", "cells")),
        P(("dp", "cells")),
    )
    return jax.shard_map(
        on_device,
        mesh=mesh,
        in_specs=placed,
        out_specs=(P(("dp", "cells"), None), P("cells", None), P("cells")),
        check_vma=False,
    )
```

```python
import functools
import math

import jax
import jax.numpy as jnp
from jax import lax
from jax.experimental import pallas as pl
from jax.experimental.pallas import tpu as pltpu
from jax.sharding import PartitionSpec as P

def code(value):
    top = jnp.maximum(jnp.max(jnp.abs(value), axis=0, keepdims=True), 1e-30)
    whole = jnp.round(value * (32767.0 / top))
    return whole.astype(jnp.int32).astype(jnp.int16), top * (1.0 / 32767.0)


def decode(whole, unit):
    return whole.astype(jnp.int32).astype(jnp.float32) * unit


def fused(
    n_cells, ndata, units,
    slots, live, jac, basis, weights, residual,
    jq, system, rhs,
    g1, g2, g3, sel, xq, xs, xrq, xrs, zrq, zrs, acc, uq, us, u, v,
    gram, gq, gs, gxq, gxs, gzq, gzs, vx, vxr, vzr, sysb,
    b_s, b_r, x_s, x_r, z_s, z_r, u_s, u_r, v_s, v_r,
    gx_s, gx_r, gz_s, gz_r, vx_s, vx_r, vz_s, vz_r, s_s, s_r,
):
    f32 = jnp.float32
    half = n_cells // 2
    tile = jac.shape[1]
    slot_count = jac.shape[2] // tile
    width = basis.shape[2]
    own_rows = gxq.shape[1]
    pieces = width // 128
    me, cell = lax.axis_index("dp"), lax.axis_index("cells")
    core, y = me % 2, me // 2
    core_peer = y * 2 + 1 - core
    y_peer = (1 - y) * 2 + core
    far_peer = (1 - y) * 2 + 1 - core
    sources = (me, core_peer, y_peer, far_peer)
    y_sources = (y_peer, far_peer, me, core_peer)
    x, line = cell % 2, cell // 2
    x_cell = line * 2 + 1 - x

    def remote(src, dst, send, recv, dp, to_cell):
        return pltpu.make_async_remote_copy(
            src_ref=src, dst_ref=dst, send_sem=send, recv_sem=recv,
            device_id=(dp, to_cell), device_id_type=pl.DeviceIdType.MESH,
        )

    def pair(src, dst, send, recv, at, to, dp, to_cell):
        return [
            remote(src[i], dst[i], send.at[(i, *at)], recv.at[(i, *to)], dp, to_cell)
            for i in range(2)
        ]

    def each(verb, copies):
        for copy in copies:
            getattr(copy, verb)()

    def lanes(source, unit=None):
        first, size = (0, width) if unit is None else units[unit][1:]
        return pl.ds(pl.multiple_of(source * width + first, 128), size)

    barrier = pltpu.get_barrier_semaphore()
    for dp, to_cell in ((core_peer, cell), (y_peer, cell), (me, x_cell)):
        pl.semaphore_signal(
            barrier, inc=1, device_id=(dp, to_cell), device_id_type=pl.DeviceIdType.MESH
        )

    @pl.loop(1, half)
    def _(k):
        pl.semaphore_signal(
            barrier, inc=1, device_id=(me, (line + k) % half * 2 + x),
            device_id_type=pl.DeviceIdType.MESH,
        )

    pl.semaphore_wait(barrier, 3 + half - 1)

    def y_piece(p):
        at = (slice(None), slice(None), pl.ds(p * 128, 128))
        return remote(
            basis.at[at], g2[p], b_s.at[1 + p], b_r.at[1 + p], y_peer, cell
        )

    def on_piece(p):
        return remote(
            g2[p], g3[p], b_s.at[1 + pieces + p], b_r.at[1 + pieces + p], core_peer, cell
        )

    to_core = remote(basis, g1, b_s.at[0], b_r.at[0], core_peer, cell)
    for p in range(pieces):
        y_piece(p).start()
    to_core.start()

    def block_dot(n, b):
        r, first, size = units[n]
        held = (basis, g1)[r] if r < 2 else (g2, g3)[r - 2][first // 128]
        for t in range(slot_count):
            rows = held[slots[b, t]]
            keep = jnp.minimum(jnp.maximum(live[b, 0] - t, 0), 1).astype(f32)
            sel[t * tile:(t + 1) * tile, 0:size] = rows * keep.astype(rows.dtype)
        return jnp.dot(jac[b], sel[:, 0:size], preferred_element_type=f32)

    def part(refs, n, j):
        r, first, size = units[n]
        return [ref.at[r, j, :, first:first + size] for ref in refs]

    def x_copy(n, j):
        return pair(
            part((xq, xs), n, j), part((xrq, xrs), n, j), x_s, x_r, (n, j), (n, j), me, x_cell
        )

    def z_copy(n, j, slot):
        return pair(
            part((xrq, xrs), n, j), part((zrq, zrs), n, slot),
            z_s, z_r, (n, j), (n, slot), me, 2 * j + x,
        )

    def send_x(n):
        r, first, size = units[n]

        @pl.loop(0, half)
        def _(j):
            value, unit = code(block_dot(n, 2 * j + 1 - x))
            xq[r, j, :, first:first + size] = value
            xs[r, j, :, first:first + size] = unit
            each("start", x_copy(n, j))

    def send_z(n):
        r, first, size = units[n]
        cols = slice(first, first + size)

        def total(j):
            value = block_dot(n, 2 * j + x)
            each("wait_recv", x_copy(n, j))
            return value + decode(xrq[r, j, :, cols], xrs[r, j, :, cols])

        @pl.loop(1, half)
        def _(k):
            j = (line + k) % half
            value, unit = code(total(j))
            xrq[r, j, :, cols] = value
            xrs[r, j, :, cols] = unit
            each("start", z_copy(n, j, line))

        acc[r, :, cols] = total(line)

    def pass_on(p):
        y_piece(p).wait_recv()
        on_piece(p).start()

    square = (tile, tile)
    wcol = jnp.transpose(jnp.broadcast_to(jnp.sqrt(weights[...]), square))[:, 0:1]
    rcol = jnp.transpose(jnp.broadcast_to(weights[...] * residual[...], square))[:, 0:1]

    def u_part(slot, cols):
        return [uq.at[slot, :, cols], us.at[slot, :, cols]]

    def u_copy(n, to):
        cols = lanes(sources[units[n][0]], n)
        return pair(
            u_part(0, cols), u_part(1 + to, cols), u_s, u_r, (to, n), (to, n),
            (core_peer, y_peer)[to], cell,
        )

    def u_on(n):
        cols = lanes(y_sources[units[n][0]], n)
        return pair(
            u_part(2, cols), u_part(3, cols), u_s, u_r, (2, n), (2, n), core_peer, cell
        )

    def keep_halves(slot, cols, value):
        high = value.astype(jnp.bfloat16)
        at = slice(slot * tile, (slot + 1) * tile)
        u[0, at, cols] = high
        u[1, at, cols] = (value - high.astype(f32)).astype(jnp.bfloat16)

    def finish_rows(n):
        r, first, size = units[n]
        cols = slice(first, first + size)

        @pl.loop(1, half)
        def _(k):
            j = (line + k) % half
            each("wait_recv", z_copy(n, j, j))
            acc[r, :, cols] = acc[r, :, cols] + decode(
                zrq[r, j, :, cols], zrs[r, j, :, cols]
            )

        total = acc[r, :, cols]
        out = lanes(sources[r], n)
        jq[:, out] = total
        scaled = total * wcol
        value, unit = code(scaled)
        uq[0, :, out] = value
        us[0, :, out] = unit
        each("start", u_copy(n, 1))
        each("start", u_copy(n, 0))
        keep_halves(0, out, scaled)
        v[0, :, out] = jnp.sum((total * rcol).reshape(tile // 8, 8, size), axis=0)

    def pass_rows_on(n):
        each("wait_recv", u_copy(n, 1))
        each("start", u_on(n))

    send_x(0)
    to_core.wait_recv()
    send_x(1)
    for p in range(pieces):
        pass_on(p)
        send_x(2 + 2 * p)
        send_z(2 * p)
        if p == pieces - 1:
            finish_rows(0)
        on_piece(p).wait_recv()
        send_x(3 + 2 * p)
        send_z(2 * p + 1)
    finish_rows(1)
    send_z(2 * pieces)
    send_z(2 * pieces + 1)
    pass_rows_on(0)
    pass_rows_on(1)
    for n in range(2, 2 + 2 * pieces):
        finish_rows(n)

    v_core = remote(v.at[0], v.at[1], v_s.at[0], v_r.at[0], core_peer, cell)
    v_y = remote(v.at[0], v.at[2], v_s.at[1], v_r.at[1], y_peer, cell)
    v_on = remote(v.at[2], v.at[3], v_s.at[2], v_r.at[2], core_peer, cell)
    v_y.start()
    v_core.start()

    def take(slot, source, n):
        cols = lanes(source, n)
        keep_halves(slot, cols, decode(uq[slot, :, cols], us[slot, :, cols]))

    for n in range(len(units)):
        r = units[n][0]
        if n >= 2:
            pass_rows_on(n)
        each("wait_recv", u_copy(n, 0))
        take(1, (core_peer, me, far_peer, y_peer)[r], n)
        take(2, y_sources[r], n)
    v_y.wait_recv()
    v_on.start()
    for n in range(len(units)):
        each("wait_recv", u_on(n))
        take(3, (far_peer, y_peer, core_peer, me)[units[n][0]], n)
    v_core.wait_recv()
    v_on.wait_recv()

    vx_copy = remote(vx.at[0], vxr, vx_s, vx_r, me, x_cell)
    vx[0] = v[0] + v[1] + v[2] + v[3]
    vx_copy.start()

    m_tile = 256

    @pl.loop(0, gram.shape[0] // m_tile)
    def _(m):
        at = pl.ds(pl.multiple_of(m * m_tile, m_tile), m_tile)

        def product(a, b):
            return lax.dot_general(
                u[a, :, at], u[b, :, lanes(me)], (((0,), (0,)), ((), ())),
                preferred_element_type=f32,
            )

        gram[at, :] = (product(0, 0) + (product(0, 1) + product(1, 0))) / ndata

    def rows_of(c):
        return pl.ds(pl.multiple_of(c * own_rows, 8), own_rows)

    def gx_copy(j):
        return pair(
            (gq.at[j], gs.at[j]), (gxq.at[j], gxs.at[j]), gx_s, gx_r, (j,), (j,), me, x_cell
        )

    def gz_copy(j, slot):
        return pair(
            (gxq.at[j], gxs.at[j]), (gzq.at[slot], gzs.at[slot]), gz_s, gz_r, (j,), (slot,),
            me, 2 * j + x,
        )

    def vz_copy(j, slot):
        return remote(vx.at[1], vzr.at[slot], vz_s.at[j], vz_r.at[slot], me, 2 * j + x)

    @pl.loop(1, half + 1)
    def _(k):
        j = (line + k) % half
        gq[j], gs[j] = code(gram[rows_of(2 * j + 1 - x), :])
        each("start", gx_copy(j))

    vx_copy.wait_recv()
    vx[1] = vx[0] + vxr[...]

    @pl.loop(1, half)
    def _(k):
        vz_copy((line + k) % half, line).start()

    @pl.loop(1, half)
    def _(k):
        j = (line + k) % half
        each("wait_recv", gx_copy(j))
        gxq[j], gxs[j] = code(decode(gxq[j], gxs[j]) + gram[rows_of(2 * j + x), :])
        each("start", gz_copy(j, line))

    each("wait_recv", gx_copy(line))
    sysb[0] = decode(gxq[line], gxs[line]) + gram[rows_of(cell), :]
    vx[2] = vx[1]

    @pl.loop(1, half)
    def _(k):
        j = (line + k) % half
        vz_copy(j, j).wait_recv()
        vx[2] = vx[2] + vzr[j]
        each("wait_recv", gz_copy(j, j))
        sysb[0] = sysb[0] + decode(gzq[j], gzs[j])

    s_y = remote(sysb.at[0], sysb.at[2], s_s.at[1], s_r.at[1], y_peer, cell)
    s_core = remote(sysb.at[0], sysb.at[1], s_s.at[0], s_r.at[0], core_peer, cell)
    s_on = remote(sysb.at[2], sysb.at[3], s_s.at[2], s_r.at[2], core_peer, cell)
    s_y.start()
    s_core.start()
    rhs[...] = jnp.sum(vx[2], axis=0, keepdims=True) / math.sqrt(ndata)

    def finish(r):
        shape = (own_rows, width)
        row = lax.broadcasted_iota(jnp.int32, shape, 0) + cell * own_rows
        column = lax.broadcasted_iota(jnp.int32, shape, 1) + sources[r] * width
        system[:, lanes(sources[r])] = sysb[r] + (row == column).astype(f32)

    finish(0)
    s_core.wait_recv()
    finish(1)
    s_y.wait_recv()
    s_on.start()
    finish(2)
    s_on.wait_recv()
    finish(3)

    to_core.wait_send()
    for p in range(pieces):
        y_piece(p).wait_send()
        on_piece(p).wait_send()
    for n in range(len(units)):
        each("wait_send", u_copy(n, 0) + u_copy(n, 1) + u_on(n))
    each("wait_send", (v_core, v_y, v_on, vx_copy, s_y, s_core, s_on))

    @pl.loop(1, half + 1)
    def _(k):
        j = (line + k) % half
        for n in range(len(units)):
            each("wait_send", x_copy(n, j))
        each("wait_send", gx_copy(j))

    @pl.loop(1, half)
    def _(k):
        j = (line + k) % half
        for n in range(len(units)):
            each("wait_send", z_copy(n, j, line))
        each("wait_send", gz_copy(j, line))
        vz_copy(j, line).wait_send()


def on_device(jac_blocks, slot_cell_blocks, live_counts, eigen_basis, weights, residual):
    n_cells = lax.axis_size("cells")
    n_groups = lax.axis_size("dp")
    half = n_cells // 2
    tile = jac_blocks.shape[1]
    depth, width = eigen_basis.shape
    full = width * n_groups
    rows_here = full // n_cells
    ndata = weights.shape[0] * n_cells * n_groups
    assert n_groups == 4 and n_cells % 2 == 0 and width % 128 == 0
    assert jac_blocks.shape[0] == n_cells and weights.shape[0] == tile
    units = [(0, 0, width), (1, 0, width)]
    for p in range(width // 128):
        units += [(2, p * 128, 128), (3, p * 128, 128)]
    f32, bf16, i16 = jnp.float32, jnp.bfloat16, jnp.int16
    vmem, smem = (pl.BlockSpec(memory_space=s) for s in (pltpu.VMEM, pltpu.SMEM))

    def sems(*shape):
        return [pltpu.SemaphoreType.DMA(shape)] * 2

    def coded(*lead, rows, columns):
        return [pltpu.VMEM((*lead, rows, columns), i16), pltpu.VMEM((*lead, 1, columns), f32)]

    chunk = pltpu.VMEM((depth // tile, tile, width), bf16)
    piece = pltpu.VMEM((depth // tile, tile, 128), bf16)
    jq, system, rhs = pl.pallas_call(
        functools.partial(fused, n_cells, ndata, tuple(units)),
        out_shape=(
            jax.ShapeDtypeStruct((tile, full), f32),
            jax.ShapeDtypeStruct((rows_here, full), f32),
            jax.ShapeDtypeStruct((1, full), f32),
        ),
        in_specs=[smem, smem, vmem, vmem, vmem, vmem],
        out_specs=(vmem, vmem, vmem),
        scratch_shapes=[
            chunk, (piece,) * (width // 128), (piece,) * (width // 128),
            pltpu.VMEM((jac_blocks.shape[2], width), bf16),
            *coded(4, half, rows=tile, columns=width),
            *coded(4, half, rows=tile, columns=width),
            *coded(4, half, rows=tile, columns=width),
            pltpu.VMEM((4, tile, width), f32),
            *coded(4, rows=tile, columns=full),
            pltpu.VMEM((2, 4 * tile, full), bf16),
            pltpu.VMEM((4, 8, full), f32),
            pltpu.VMEM((full, width), f32),
            *coded(half, rows=rows_here, columns=width),
            *coded(half, rows=rows_here, columns=width),
            *coded(half, rows=rows_here, columns=width),
            pltpu.VMEM((3, 8, full), f32),
            pltpu.VMEM((8, full), f32),
            pltpu.VMEM((half, 8, full), f32),
            pltpu.VMEM((4, rows_here, width), f32),
            *sems(1 + 2 * (width // 128)), *sems(2, len(units), half), *sems(2, len(units), half),
            *sems(2, 3, len(units)), *sems(3),
            *sems(2, half), *sems(2, half), *sems(), *sems(half), *sems(3),
        ],
        compiler_params=pltpu.CompilerParams(
            collective_id=0, has_side_effects=True, vmem_limit_bytes=60 * 1024 * 1024
        ),
    )(
        slot_cell_blocks, live_counts, jac_blocks,
        eigen_basis.reshape(depth // tile, tile, width), weights[None], residual[None],
    )
    start = lax.axis_index("cells") * rows_here
    return jq, system, lax.dynamic_slice(rhs[0], (start,), (rows_here,))


def solution(mesh):
    placed = (
        P("dp", None, "cells"),
        P("dp", "cells"),
        P("dp", "cells"),
        P("cells", "dp"),
        P(("dp", "cells")),
        P(("dp", "cells")),
    )
    return jax.shard_map(
        on_device,
        mesh=mesh,
        in_specs=placed,
        out_specs=(P(("dp", "cells"), None), P("cells", None), P("cells")),
        check_vma=False,
    )
```

```python
import functools
import math

import jax
import jax.numpy as jnp
from jax import lax
from jax.experimental import pallas as pl
from jax.experimental.pallas import tpu as pltpu
from jax.sharding import PartitionSpec as P

def code(value):
    top = jnp.maximum(jnp.max(jnp.abs(value), axis=0, keepdims=True), 1e-30)
    whole = jnp.round(value * (32767.0 / top))
    return whole.astype(jnp.int32).astype(jnp.int16), top * (1.0 / 32767.0)


def decode(whole, unit):
    return whole.astype(jnp.int32).astype(jnp.float32) * unit


def fused(
    n_cells, ndata, units,
    slots, live, jac, basis, weights, residual,
    jq, system, rhs,
    g1, g2, g3, xq, xs, xrq, xrs, zrq, zrs, acc, uq, us, u, v,
    gram, gq, gs, gxq, gxs, gzq, gzs, vx, vxr, vzr, sysb,
    b_s, b_r, x_s, x_r, z_s, z_r, u_s, u_r, v_s, v_r,
    gx_s, gx_r, gz_s, gz_r, vx_s, vx_r, vz_s, vz_r, s_s, s_r,
):
    f32 = jnp.float32
    half = n_cells // 2
    tile = jac.shape[1]
    slot_count = jac.shape[2] // tile
    width = basis.shape[2]
    own_rows = gxq.shape[1]
    pieces = width // 128
    me, cell = lax.axis_index("dp"), lax.axis_index("cells")
    core, y = me % 2, me // 2
    core_peer = y * 2 + 1 - core
    y_peer = (1 - y) * 2 + core
    far_peer = (1 - y) * 2 + 1 - core
    sources = (me, core_peer, y_peer, far_peer)
    y_sources = (y_peer, far_peer, me, core_peer)
    x, line = cell % 2, cell // 2
    x_cell = line * 2 + 1 - x

    def remote(src, dst, send, recv, dp, to_cell):
        return pltpu.make_async_remote_copy(
            src_ref=src, dst_ref=dst, send_sem=send, recv_sem=recv,
            device_id=(dp, to_cell), device_id_type=pl.DeviceIdType.MESH,
        )

    def pair(src, dst, send, recv, at, to, dp, to_cell):
        return [
            remote(src[i], dst[i], send.at[(i, *at)], recv.at[(i, *to)], dp, to_cell)
            for i in range(2)
        ]

    def each(verb, copies):
        for copy in copies:
            getattr(copy, verb)()

    def lanes(source, first=0, size=width):
        return pl.ds(pl.multiple_of(source * width + first, 128), size)

    def runs(n):
        at = 0
        for r, first, size in units[n]:
            yield r, first, size, slice(at, at + size)
            at += size

    def span(n):
        sizes = [sum(size for _, _, size in unit) for unit in units]
        return slice(sum(sizes[:n]), sum(sizes[:n + 1]))

    barrier = pltpu.get_barrier_semaphore()
    for dp, to_cell in ((core_peer, cell), (y_peer, cell), (me, x_cell)):
        pl.semaphore_signal(
            barrier, inc=1, device_id=(dp, to_cell), device_id_type=pl.DeviceIdType.MESH
        )

    @pl.loop(1, half)
    def _(k):
        pl.semaphore_signal(
            barrier, inc=1, device_id=(me, (line + k) % half * 2 + x),
            device_id_type=pl.DeviceIdType.MESH,
        )

    pl.semaphore_wait(barrier, 3 + half - 1)

    def y_piece(p):
        at = (slice(None), slice(None), pl.ds(p * 128, 128))
        return remote(
            basis.at[at], g2[p], b_s.at[1 + p], b_r.at[1 + p], y_peer, cell
        )

    def on_piece(p):
        return remote(
            g2[p], g3[p], b_s.at[1 + pieces + p], b_r.at[1 + pieces + p], core_peer, cell
        )

    to_core = remote(basis, g1, b_s.at[0], b_r.at[0], core_peer, cell)
    for p in range(pieces):
        y_piece(p).start()
    to_core.start()

    def block_dot(n, b):
        total = None
        for t in range(0, slot_count, 2):
            rows = []
            for i in (t, t + 1):
                keep = jnp.minimum(jnp.maximum(live[b, 0] - i, 0), 1).astype(f32)
                cut = [
                    (basis, g1)[r][slots[b, i]] if r < 2
                    else (g2, g3)[r - 2][first // 128][slots[b, i]]
                    for r, first, _ in units[n]
                ]
                row = cut[0] if len(cut) == 1 else jnp.concatenate(cut, axis=1)
                rows.append(row * keep.astype(row.dtype))
            term = jnp.dot(
                jac[b, :, t * tile:(t + 2) * tile], jnp.concatenate(rows, axis=0),
                preferred_element_type=f32,
            )
            total = term if total is None else total + term
        return total

    def part(refs, n, j):
        return [ref.at[j, :, span(n)] for ref in refs]

    def x_copy(n, j):
        return pair(
            part((xq, xs), n, j), part((xrq, xrs), n, j), x_s, x_r, (n, j), (n, j), me, x_cell
        )

    def z_copy(n, j, slot):
        return pair(
            part((xrq, xrs), n, j), part((zrq, zrs), n, slot),
            z_s, z_r, (n, j), (n, slot), me, 2 * j + x,
        )

    def send_x(n):
        cols = span(n)
        for k in range(1, half + 1) if half <= 4 else (None,):
            def one(k):
                j = (line + k) % half
                xq[j, :, cols], xs[j, :, cols] = code(block_dot(n, 2 * j + 1 - x))
                each("start", x_copy(n, j))

            one(k) if k is not None else pl.loop(1, half + 1)(one)

    def send_z(n):
        cols = span(n)

        def total(j):
            value = block_dot(n, 2 * j + x)
            each("wait_recv", x_copy(n, j))
            return value + decode(xrq[j, :, cols], xrs[j, :, cols])

        for k in range(1, half) if half <= 4 else (None,):
            def one(k):
                j = (line + k) % half
                xrq[j, :, cols], xrs[j, :, cols] = code(total(j))
                each("start", z_copy(n, j, line))

            one(k) if k is not None else pl.loop(1, half)(one)

        acc[:, cols] = total(line)

    def pass_on(p):
        y_piece(p).wait_recv()
        on_piece(p).start()

    square = (tile, tile)
    wcol = jnp.transpose(jnp.broadcast_to(jnp.sqrt(weights[...]), square))[:, 0:1]
    rcol = jnp.transpose(jnp.broadcast_to(weights[...] * residual[...], square))[:, 0:1]

    def u_part(slot, cols):
        return [uq.at[slot, :, cols], us.at[slot, :, cols]]

    def u_copy(n, to):
        cols = span(n)
        return pair(
            u_part(0, cols), u_part(1 + to, cols), u_s, u_r, (to, n), (to, n),
            (core_peer, y_peer)[to], cell,
        )

    def u_on(n):
        cols = span(n)
        return pair(
            u_part(2, cols), u_part(3, cols), u_s, u_r, (2, n), (2, n), core_peer, cell
        )

    def keep_halves(slot, cols, value):
        high = value.astype(jnp.bfloat16)
        at = slice(slot * tile, (slot + 1) * tile)
        u[0, at, cols] = high
        u[1, at, cols] = (value - high.astype(f32)).astype(jnp.bfloat16)

    def finish_rows(n):
        cols = span(n)

        @pl.loop(1, half)
        def _(k):
            j = (line + k) % half
            each("wait_recv", z_copy(n, j, j))
            acc[:, cols] = acc[:, cols] + decode(zrq[j, :, cols], zrs[j, :, cols])

        total = acc[:, cols]
        scaled = total * wcol
        uq[0, :, cols], us[0, :, cols] = code(scaled)
        each("start", u_copy(n, 1))
        each("start", u_copy(n, 0))
        misfit = jnp.sum((total * rcol).reshape(tile // 8, 8, total.shape[1]), axis=0)
        for r, first, size, at in runs(n):
            out = lanes(sources[r], first, size)
            jq[:, out] = total[:, at]
            v[0, :, out] = misfit[:, at]
            keep_halves(0, out, scaled[:, at])

    def pass_rows_on(n):
        each("wait_recv", u_copy(n, 1))
        each("start", u_on(n))

    send_x(0)
    to_core.wait_recv()
    send_x(1)
    for p in range(pieces):
        pass_on(p)
        if p < 2:
            send_z(p)
        else:
            send_z(p)
            finish_rows(p - 2)
        on_piece(p).wait_recv()
        send_x(2 + p)
    send_z(pieces)
    finish_rows(pieces - 2)
    send_z(pieces + 1)
    for n in range(pieces - 1, pieces + 2):
        pass_rows_on(n - pieces + 1)
        finish_rows(n)

    v_core = remote(v.at[0], v.at[1], v_s.at[0], v_r.at[0], core_peer, cell)
    v_y = remote(v.at[0], v.at[2], v_s.at[1], v_r.at[1], y_peer, cell)
    v_on = remote(v.at[2], v.at[3], v_s.at[2], v_r.at[2], core_peer, cell)
    v_y.start()
    v_core.start()

    def take(slot, order, n):
        value = decode(uq[slot, :, span(n)], us[slot, :, span(n)])
        for r, first, size, at in runs(n):
            keep_halves(slot, lanes(order[r], first, size), value[:, at])

    for n in range(len(units)):
        if n >= 3:
            pass_rows_on(n)
        each("wait_recv", u_copy(n, 0))
        take(1, (core_peer, me, far_peer, y_peer), n)
        take(2, y_sources, n)
    v_y.wait_recv()
    v_on.start()
    for n in range(len(units)):
        each("wait_recv", u_on(n))
        take(3, (far_peer, y_peer, core_peer, me), n)
    v_core.wait_recv()
    v_on.wait_recv()

    vx_copy = remote(vx.at[0], vxr, vx_s, vx_r, me, x_cell)
    vx[0] = v[0] + v[1] + v[2] + v[3]
    vx_copy.start()

    m_tile = 256

    @pl.loop(0, gram.shape[0] // m_tile)
    def _(m):
        at = pl.ds(pl.multiple_of(m * m_tile, m_tile), m_tile)

        def product(a, b):
            return lax.dot_general(
                u[a, :, at], u[b, :, lanes(me)], (((0,), (0,)), ((), ())),
                preferred_element_type=f32,
            )

        gram[at, :] = (product(0, 0) + (product(0, 1) + product(1, 0))) / ndata

    def rows_of(c):
        return pl.ds(pl.multiple_of(c * own_rows, 8), own_rows)

    def gx_copy(j):
        return pair(
            (gq.at[j], gs.at[j]), (gxq.at[j], gxs.at[j]), gx_s, gx_r, (j,), (j,), me, x_cell
        )

    def gz_copy(j, slot):
        return pair(
            (gxq.at[j], gxs.at[j]), (gzq.at[slot], gzs.at[slot]), gz_s, gz_r, (j,), (slot,),
            me, 2 * j + x,
        )

    def vz_copy(j, slot):
        return remote(vx.at[1], vzr.at[slot], vz_s.at[j], vz_r.at[slot], me, 2 * j + x)

    @pl.loop(1, half + 1)
    def _(k):
        j = (line + k) % half
        gq[j], gs[j] = code(gram[rows_of(2 * j + 1 - x), :])
        each("start", gx_copy(j))

    vx_copy.wait_recv()
    vx[1] = vx[0] + vxr[...]

    @pl.loop(1, half)
    def _(k):
        vz_copy((line + k) % half, line).start()

    @pl.loop(1, half)
    def _(k):
        j = (line + k) % half
        each("wait_recv", gx_copy(j))
        gxq[j], gxs[j] = code(decode(gxq[j], gxs[j]) + gram[rows_of(2 * j + x), :])
        each("start", gz_copy(j, line))

    each("wait_recv", gx_copy(line))
    sysb[0] = decode(gxq[line], gxs[line]) + gram[rows_of(cell), :]
    vx[2] = vx[1]

    @pl.loop(1, half)
    def _(k):
        j = (line + k) % half
        vz_copy(j, j).wait_recv()
        vx[2] = vx[2] + vzr[j]
        each("wait_recv", gz_copy(j, j))
        sysb[0] = sysb[0] + decode(gzq[j], gzs[j])

    s_y = remote(sysb.at[0], sysb.at[2], s_s.at[1], s_r.at[1], y_peer, cell)
    s_core = remote(sysb.at[0], sysb.at[1], s_s.at[0], s_r.at[0], core_peer, cell)
    s_on = remote(sysb.at[2], sysb.at[3], s_s.at[2], s_r.at[2], core_peer, cell)
    s_y.start()
    s_core.start()
    rhs[...] = jnp.sum(vx[2], axis=0, keepdims=True) / math.sqrt(ndata)

    def finish(r):
        shape = (own_rows, width)
        row = lax.broadcasted_iota(jnp.int32, shape, 0) + cell * own_rows
        column = lax.broadcasted_iota(jnp.int32, shape, 1) + sources[r] * width
        system[:, lanes(sources[r])] = sysb[r] + (row == column).astype(f32)

    finish(0)
    s_core.wait_recv()
    finish(1)
    s_y.wait_recv()
    s_on.start()
    finish(2)
    s_on.wait_recv()
    finish(3)

    to_core.wait_send()
    for p in range(pieces):
        y_piece(p).wait_send()
        on_piece(p).wait_send()
    for n in range(len(units)):
        each("wait_send", u_copy(n, 0) + u_copy(n, 1) + u_on(n))
    each("wait_send", (v_core, v_y, v_on, vx_copy, s_y, s_core, s_on))

    @pl.loop(1, half + 1)
    def _(k):
        j = (line + k) % half
        for n in range(len(units)):
            each("wait_send", x_copy(n, j))
        each("wait_send", gx_copy(j))

    @pl.loop(1, half)
    def _(k):
        j = (line + k) % half
        for n in range(len(units)):
            each("wait_send", z_copy(n, j, line))
        each("wait_send", gz_copy(j, line))
        vz_copy(j, line).wait_send()


def on_device(jac_blocks, slot_cell_blocks, live_counts, eigen_basis, weights, residual):
    n_cells = lax.axis_size("cells")
    n_groups = lax.axis_size("dp")
    half = n_cells // 2
    tile = jac_blocks.shape[1]
    depth, width = eigen_basis.shape
    full = width * n_groups
    rows_here = full // n_cells
    ndata = weights.shape[0] * n_cells * n_groups
    assert n_groups == 4 and n_cells % 2 == 0 and width % 128 == 0
    assert jac_blocks.shape[0] == n_cells and weights.shape[0] == tile
    units = [((0, 0, width),), ((1, 0, width),)]
    units += [((2, p * 128, 128), (3, p * 128, 128)) for p in range(width // 128)]
    f32, bf16, i16 = jnp.float32, jnp.bfloat16, jnp.int16
    vmem, smem = (pl.BlockSpec(memory_space=s) for s in (pltpu.VMEM, pltpu.SMEM))

    def sems(*shape):
        return [pltpu.SemaphoreType.DMA(shape)] * 2

    def coded(*lead, rows, columns):
        return [pltpu.VMEM((*lead, rows, columns), i16), pltpu.VMEM((*lead, 1, columns), f32)]

    chunk = pltpu.VMEM((depth // tile, tile, width), bf16)
    piece = pltpu.VMEM((depth // tile, tile, 128), bf16)
    jq, system, rhs = pl.pallas_call(
        functools.partial(fused, n_cells, ndata, tuple(units)),
        out_shape=(
            jax.ShapeDtypeStruct((tile, full), f32),
            jax.ShapeDtypeStruct((rows_here, full), f32),
            jax.ShapeDtypeStruct((1, full), f32),
        ),
        in_specs=[smem, smem, vmem, vmem, vmem, vmem],
        out_specs=(vmem, vmem, vmem),
        scratch_shapes=[
            chunk, (piece,) * (width // 128), (piece,) * (width // 128),
            *coded(half, rows=tile, columns=full),
            *coded(half, rows=tile, columns=full),
            *coded(half, rows=tile, columns=full),
            pltpu.VMEM((tile, full), f32),
            *coded(4, rows=tile, columns=full),
            pltpu.VMEM((2, 4 * tile, full), bf16),
            pltpu.VMEM((4, 8, full), f32),
            pltpu.VMEM((full, width), f32),
            *coded(half, rows=rows_here, columns=width),
            *coded(half, rows=rows_here, columns=width),
            *coded(half, rows=rows_here, columns=width),
            pltpu.VMEM((3, 8, full), f32),
            pltpu.VMEM((8, full), f32),
            pltpu.VMEM((half, 8, full), f32),
            pltpu.VMEM((4, rows_here, width), f32),
            *sems(1 + 2 * (width // 128)), *sems(2, len(units), half), *sems(2, len(units), half),
            *sems(2, 3, len(units)), *sems(3),
            *sems(2, half), *sems(2, half), *sems(), *sems(half), *sems(3),
        ],
        compiler_params=pltpu.CompilerParams(
            collective_id=0, has_side_effects=True, vmem_limit_bytes=60 * 1024 * 1024
        ),
    )(
        slot_cell_blocks, live_counts, jac_blocks,
        eigen_basis.reshape(depth // tile, tile, width), weights[None], residual[None],
    )
    start = lax.axis_index("cells") * rows_here
    return jq, system, lax.dynamic_slice(rhs[0], (start,), (rows_here,))


def solution(mesh):
    placed = (
        P("dp", None, "cells"),
        P("dp", "cells"),
        P("dp", "cells"),
        P("cells", "dp"),
        P(("dp", "cells")),
        P(("dp", "cells")),
    )
    return jax.shard_map(
        on_device,
        mesh=mesh,
        in_specs=placed,
        out_specs=(P(("dp", "cells"), None), P("cells", None), P("cells")),
        check_vma=False,
    )
```

```python
import functools
import math

import jax
import jax.numpy as jnp
from jax import lax
from jax.experimental import pallas as pl
from jax.experimental.pallas import tpu as pltpu
from jax.sharding import PartitionSpec as P

def code(value):
    top = jnp.maximum(jnp.max(jnp.abs(value), axis=0, keepdims=True), 1e-30)
    whole = jnp.round(value * (32767.0 / top))
    return whole.astype(jnp.int32).astype(jnp.int16), top * (1.0 / 32767.0)


def decode(whole, unit):
    return whole.astype(jnp.int32).astype(jnp.float32) * unit


def fused(
    n_cells, ndata, units,
    slots, live, jac, basis, weights, residual,
    jq, system, rhs,
    g1, g2, g3, sel, xq, xs, xrq, xrs, zrq, zrs, acc, uq, us, u, v,
    gram, gq, gs, gxq, gxs, gzq, gzs, vx, vxr, vzr, sysb, sq, su,
    b_s, b_r, x_s, x_r, z_s, z_r, u_s, u_r, v_s, v_r,
    gx_s, gx_r, gz_s, gz_r, vx_s, vx_r, vz_s, vz_r, s_s, s_r,
):
    f32 = jnp.float32
    half = n_cells // 2
    tile = jac.shape[1]
    slot_count = jac.shape[2] // tile
    width = basis.shape[2]
    own_rows = gxq.shape[1]
    pieces = width // 128
    me, cell = lax.axis_index("dp"), lax.axis_index("cells")
    core, y = me % 2, me // 2
    core_peer = y * 2 + 1 - core
    y_peer = (1 - y) * 2 + core
    far_peer = (1 - y) * 2 + 1 - core
    sources = (me, core_peer, y_peer, far_peer)
    y_sources = (y_peer, far_peer, me, core_peer)
    x, line = cell % 2, cell // 2
    x_cell = line * 2 + 1 - x

    def remote(src, dst, send, recv, dp, to_cell):
        return pltpu.make_async_remote_copy(
            src_ref=src, dst_ref=dst, send_sem=send, recv_sem=recv,
            device_id=(dp, to_cell), device_id_type=pl.DeviceIdType.MESH,
        )

    def pair(src, dst, send, recv, at, to, dp, to_cell):
        return [
            remote(src[i], dst[i], send.at[(i, *at)], recv.at[(i, *to)], dp, to_cell)
            for i in range(2)
        ]

    def each(verb, copies):
        for copy in copies:
            getattr(copy, verb)()

    def lanes(source, unit=None):
        first, size = (0, width) if unit is None else units[unit][1:]
        return pl.ds(pl.multiple_of(source * width + first, 128), size)

    barrier = pltpu.get_barrier_semaphore()
    for dp, to_cell in ((core_peer, cell), (y_peer, cell), (me, x_cell)):
        pl.semaphore_signal(
            barrier, inc=1, device_id=(dp, to_cell), device_id_type=pl.DeviceIdType.MESH
        )

    @pl.loop(1, half)
    def _(k):
        pl.semaphore_signal(
            barrier, inc=1, device_id=(me, (line + k) % half * 2 + x),
            device_id_type=pl.DeviceIdType.MESH,
        )

    pl.semaphore_wait(barrier, 3 + half - 1)

    def y_piece(p):
        at = (slice(None), slice(None), pl.ds(p * 128, 128))
        return remote(
            basis.at[at], g2[p], b_s.at[1 + p], b_r.at[1 + p], y_peer, cell
        )

    def on_piece(p):
        return remote(
            g2[p], g3[p], b_s.at[1 + pieces + p], b_r.at[1 + pieces + p], core_peer, cell
        )

    to_core = remote(basis, g1, b_s.at[0], b_r.at[0], core_peer, cell)
    for p in range(pieces):
        y_piece(p).start()
    to_core.start()

    def block_dot(n, b):
        r, first, size = units[n]
        held = (basis, g1)[r] if r < 2 else (g2, g3)[r - 2][first // 128]
        for t in range(slot_count):
            rows = held[slots[b, t]]
            keep = jnp.minimum(jnp.maximum(live[b] - t, 0), 1).astype(f32)
            sel[t * tile:(t + 1) * tile, 0:size] = rows * keep.astype(rows.dtype)
        return jnp.dot(jac[b], sel[:, 0:size], preferred_element_type=f32)

    def part(refs, n, j):
        r, first, size = units[n]
        return [ref.at[r, j, :, first:first + size] for ref in refs]

    def x_copy(n, j):
        return pair(
            part((xq, xs), n, j), part((xrq, xrs), n, j), x_s, x_r, (n, j), (n, j), me, x_cell
        )

    def z_copy(n, j, slot):
        return pair(
            part((xrq, xrs), n, j), part((zrq, zrs), n, slot),
            z_s, z_r, (n, j), (n, slot), me, 2 * j + x,
        )

    def send_x(n):
        r, first, size = units[n]

        @pl.loop(0, half)
        def _(j):
            value, unit = code(block_dot(n, 2 * j + 1 - x))
            xq[r, j, :, first:first + size] = value
            xs[r, j, :, first:first + size] = unit
            each("start", x_copy(n, j))

    def send_z(n):
        r, first, size = units[n]
        cols = slice(first, first + size)

        def total(j):
            value = block_dot(n, 2 * j + x)
            each("wait_recv", x_copy(n, j))
            return value + decode(xrq[r, j, :, cols], xrs[r, j, :, cols])

        @pl.loop(1, half)
        def _(k):
            j = (line + k) % half
            value, unit = code(total(j))
            xrq[r, j, :, cols] = value
            xrs[r, j, :, cols] = unit
            each("start", z_copy(n, j, line))

        acc[r, :, cols] = total(line)

    def pass_on(p):
        y_piece(p).wait_recv()
        on_piece(p).start()

    square = (tile, tile)
    wcol = jnp.transpose(jnp.broadcast_to(jnp.sqrt(weights[...]), square))[:, 0:1]
    rcol = jnp.transpose(jnp.broadcast_to(weights[...] * residual[...], square))[:, 0:1]

    def u_part(slot, cols):
        return [uq.at[slot, :, cols], us.at[slot, :, cols]]

    def u_copy(n, to):
        cols = lanes(sources[units[n][0]], n)
        return pair(
            u_part(0, cols), u_part(1 + to, cols), u_s, u_r, (to, n), (to, n),
            (core_peer, y_peer)[to], cell,
        )

    def u_on(n):
        cols = lanes(y_sources[units[n][0]], n)
        return pair(
            u_part(2, cols), u_part(3, cols), u_s, u_r, (2, n), (2, n), core_peer, cell
        )

    def keep_halves(slot, cols, value):
        high = value.astype(jnp.bfloat16)
        at = slice(slot * tile, (slot + 1) * tile)
        u[0, at, cols] = high
        u[1, at, cols] = (value - high.astype(f32)).astype(jnp.bfloat16)

    def finish_rows(n):
        r, first, size = units[n]
        cols = slice(first, first + size)

        @pl.loop(1, half)
        def _(k):
            j = (line + k) % half
            each("wait_recv", z_copy(n, j, j))
            acc[r, :, cols] = acc[r, :, cols] + decode(
                zrq[r, j, :, cols], zrs[r, j, :, cols]
            )

        total = acc[r, :, cols]
        out = lanes(sources[r], n)
        jq[:, out] = total
        scaled = total * wcol
        value, unit = code(scaled)
        uq[0, :, out] = value
        us[0, :, out] = unit
        each("start", u_copy(n, 1))
        each("start", u_copy(n, 0))
        keep_halves(0, out, scaled)
        v[0, :, out] = jnp.sum((total * rcol).reshape(tile // 8, 8, size), axis=0)

    def pass_rows_on(n):
        each("wait_recv", u_copy(n, 1))
        each("start", u_on(n))

    send_x(0)
    to_core.wait_recv()
    send_x(1)
    for p in range(pieces):
        pass_on(p)
        send_x(2 + 2 * p)
        send_z(2 * p)
        if p == pieces - 1:
            finish_rows(0)
        on_piece(p).wait_recv()
        send_x(3 + 2 * p)
        send_z(2 * p + 1)
    finish_rows(1)
    send_z(2 * pieces)
    send_z(2 * pieces + 1)
    pass_rows_on(0)
    pass_rows_on(1)
    for n in range(2, 2 + 2 * pieces):
        finish_rows(n)

    v_core = remote(v.at[0], v.at[1], v_s.at[0], v_r.at[0], core_peer, cell)
    v_y = remote(v.at[0], v.at[2], v_s.at[1], v_r.at[1], y_peer, cell)
    v_on = remote(v.at[2], v.at[3], v_s.at[2], v_r.at[2], core_peer, cell)
    v_y.start()
    v_core.start()

    def take(slot, source, n):
        cols = lanes(source, n)
        keep_halves(slot, cols, decode(uq[slot, :, cols], us[slot, :, cols]))

    for n in range(len(units)):
        r = units[n][0]
        if n >= 2:
            pass_rows_on(n)
        each("wait_recv", u_copy(n, 0))
        take(1, (core_peer, me, far_peer, y_peer)[r], n)
        take(2, y_sources[r], n)
    v_y.wait_recv()
    v_on.start()
    for n in range(len(units)):
        each("wait_recv", u_on(n))
        take(3, (far_peer, y_peer, core_peer, me)[units[n][0]], n)
    v_core.wait_recv()
    v_on.wait_recv()

    vx_copy = remote(vx.at[0], vxr, vx_s, vx_r, me, x_cell)
    vx[0] = v[0] + v[1] + v[2] + v[3]
    vx_copy.start()

    m_tile = 256

    @pl.loop(0, gram.shape[0] // m_tile)
    def _(m):
        at = pl.ds(pl.multiple_of(m * m_tile, m_tile), m_tile)

        def product(a, b):
            return lax.dot_general(
                u[a, :, at], u[b, :, lanes(me)], (((0,), (0,)), ((), ())),
                preferred_element_type=f32,
            )

        gram[at, :] = (product(0, 0) + (product(0, 1) + product(1, 0))) / ndata

    def rows_of(c):
        return pl.ds(pl.multiple_of(c * own_rows, 8), own_rows)

    def gx_copy(j):
        return pair(
            (gq.at[j], gs.at[j]), (gxq.at[j], gxs.at[j]), gx_s, gx_r, (j,), (j,), me, x_cell
        )

    def gz_copy(j, slot):
        return pair(
            (gxq.at[j], gxs.at[j]), (gzq.at[slot], gzs.at[slot]), gz_s, gz_r, (j,), (slot,),
            me, 2 * j + x,
        )

    def vz_copy(j, slot):
        return remote(vx.at[1], vzr.at[slot], vz_s.at[j], vz_r.at[slot], me, 2 * j + x)

    @pl.loop(1, half + 1)
    def _(k):
        j = (line + k) % half
        gq[j], gs[j] = code(gram[rows_of(2 * j + 1 - x), :])
        each("start", gx_copy(j))

    vx_copy.wait_recv()
    vx[1] = vx[0] + vxr[...]

    @pl.loop(1, half)
    def _(k):
        vz_copy((line + k) % half, line).start()

    @pl.loop(1, half)
    def _(k):
        j = (line + k) % half
        each("wait_recv", gx_copy(j))
        gxq[j], gxs[j] = code(decode(gxq[j], gxs[j]) + gram[rows_of(2 * j + x), :])
        each("start", gz_copy(j, line))

    each("wait_recv", gx_copy(line))
    sysb[...] = decode(gxq[line], gxs[line]) + gram[rows_of(cell), :]
    vx[2] = vx[1]

    @pl.loop(1, half)
    def _(k):
        j = (line + k) % half
        vz_copy(j, j).wait_recv()
        vx[2] = vx[2] + vzr[j]
        each("wait_recv", gz_copy(j, j))
        sysb[...] = sysb[...] + decode(gzq[j], gzs[j])

    def s_copy(i, src, dst, dp):
        return pair(
            (sq.at[src], su.at[src]), (sq.at[dst], su.at[dst]), s_s, s_r, (i,), (i,), dp, cell
        )

    sq[0], su[0] = code(sysb[...])
    s_y, s_core, s_on = s_copy(1, 0, 2, y_peer), s_copy(0, 0, 1, core_peer), s_copy(2, 2, 3, core_peer)
    each("start", s_y)
    each("start", s_core)
    misfit = jnp.sum(vx[2], axis=0, keepdims=True) / math.sqrt(ndata)
    own = jnp.zeros(rhs.shape, f32)
    for c in range(n_cells):
        own = jnp.where(cell == c, misfit[:, c * own_rows:(c + 1) * own_rows], own)
    rhs[...] = own

    def finish(r):
        shape = (own_rows, width)
        row = lax.broadcasted_iota(jnp.int32, shape, 0) + cell * own_rows
        column = lax.broadcasted_iota(jnp.int32, shape, 1) + sources[r] * width
        system[:, lanes(sources[r])] = decode(sq[r], su[r]) + (row == column).astype(f32)

    finish(0)
    each("wait_recv", s_core)
    finish(1)
    each("wait_recv", s_y)
    each("start", s_on)
    finish(2)
    each("wait_recv", s_on)
    finish(3)

    to_core.wait_send()
    for p in range(pieces):
        y_piece(p).wait_send()
        on_piece(p).wait_send()
    for n in range(len(units)):
        each("wait_send", u_copy(n, 0) + u_copy(n, 1) + u_on(n))
    each("wait_send", [v_core, v_y, v_on, vx_copy] + s_y + s_core + s_on)

    @pl.loop(1, half + 1)
    def _(k):
        j = (line + k) % half
        for n in range(len(units)):
            each("wait_send", x_copy(n, j))
        each("wait_send", gx_copy(j))

    @pl.loop(1, half)
    def _(k):
        j = (line + k) % half
        for n in range(len(units)):
            each("wait_send", z_copy(n, j, line))
        each("wait_send", gz_copy(j, line))
        vz_copy(j, line).wait_send()


def on_device(jac_blocks, slot_cell_blocks, live_counts, eigen_basis, weights, residual):
    n_cells = lax.axis_size("cells")
    n_groups = lax.axis_size("dp")
    half = n_cells // 2
    tile = jac_blocks.shape[1]
    depth, width = eigen_basis.shape
    full = width * n_groups
    rows_here = full // n_cells
    ndata = weights.shape[0] * n_cells * n_groups
    assert n_groups == 4 and n_cells % 2 == 0 and width % 128 == 0
    assert jac_blocks.shape[0] == n_cells and weights.shape[0] == tile
    units = [(0, 0, width), (1, 0, width)]
    for p in range(width // 128):
        units += [(2, p * 128, 128), (3, p * 128, 128)]
    f32, bf16, i16 = jnp.float32, jnp.bfloat16, jnp.int16
    vmem, smem = (pl.BlockSpec(memory_space=s) for s in (pltpu.VMEM, pltpu.SMEM))

    def sems(*shape):
        return [pltpu.SemaphoreType.DMA(shape)] * 2

    def coded(*lead, rows, columns):
        return [pltpu.VMEM((*lead, rows, columns), i16), pltpu.VMEM((*lead, 1, columns), f32)]

    chunk = pltpu.VMEM((depth // tile, tile, width), bf16)
    piece = pltpu.VMEM((depth // tile, tile, 128), bf16)
    jq, system, rhs = pl.pallas_call(
        functools.partial(fused, n_cells, ndata, tuple(units)),
        out_shape=(
            jax.ShapeDtypeStruct((tile, full), f32),
            jax.ShapeDtypeStruct((rows_here, full), f32),
            jax.ShapeDtypeStruct((1, rows_here), f32),
        ),
        in_specs=[smem, smem, vmem, vmem, vmem, vmem],
        out_specs=(vmem, vmem, vmem),
        scratch_shapes=[
            chunk, (piece,) * (width // 128), (piece,) * (width // 128),
            pltpu.VMEM((jac_blocks.shape[2], width), bf16),
            *coded(4, half, rows=tile, columns=width),
            *coded(4, half, rows=tile, columns=width),
            *coded(4, half, rows=tile, columns=width),
            pltpu.VMEM((4, tile, width), f32),
            *coded(4, rows=tile, columns=full),
            pltpu.VMEM((2, 4 * tile, full), bf16),
            pltpu.VMEM((4, 8, full), f32),
            pltpu.VMEM((full, width), f32),
            *coded(half, rows=rows_here, columns=width),
            *coded(half, rows=rows_here, columns=width),
            *coded(half, rows=rows_here, columns=width),
            pltpu.VMEM((3, 8, full), f32),
            pltpu.VMEM((8, full), f32),
            pltpu.VMEM((half, 8, full), f32),
            pltpu.VMEM((rows_here, width), f32),
            *coded(4, rows=rows_here, columns=width),
            *sems(1 + 2 * (width // 128)), *sems(2, len(units), half), *sems(2, len(units), half),
            *sems(2, 3, len(units)), *sems(3),
            *sems(2, half), *sems(2, half), *sems(), *sems(half), *sems(2, 3),
        ],
        compiler_params=pltpu.CompilerParams(
            collective_id=0, has_side_effects=True, vmem_limit_bytes=60 * 1024 * 1024
        ),
    )(
        slot_cell_blocks, live_counts[:, 0], jac_blocks,
        eigen_basis.reshape(depth // tile, tile, width), weights[None], residual[None],
    )
    return jq, system, rhs[0]


def solution(mesh):
    placed = (
        P("dp", None, "cells"),
        P("dp", "cells"),
        P("dp", "cells"),
        P("cells", "dp"),
        P(("dp", "cells")),
        P(("dp", "cells")),
    )
    return jax.shard_map(
        on_device,
        mesh=mesh,
        in_specs=placed,
        out_specs=(P(("dp", "cells"), None), P("cells", None), P("cells")),
        check_vma=False,
    )
```
